32 devices in a mesh: seq: 8 (over z, x), tp: 4 (over y, core).
Axes of the slice: x: 2, y: 2, z: 4, core: 2. Of those that a mesh axis runs over, the one named last changes fastest.
Arguments:
- hidden: bfloat16 [2048, 8192], P('seq', 'tp'), may hold values from -6 to 6
- norm_gain: float32 [8192], replicated, may hold values from 0.1 to 1.9
- w_query: bfloat16 [8192, 4096], P('seq', 'tp')
- w_key: bfloat16 [8192, 512], P('seq', 'tp')
- value_weight: bfloat16 [8192, 512], P('seq', 'tp'), may hold values from -0.0625 to 0.0625
- vertical_blocks: int32 [32, 16], replicated, may hold values from 0 to 31, as said below
- slash_offsets: int32 [32, 16], replicated, may hold values from 0 to 31, as said below
- counts: int32 [32, 2], replicated, may hold values from 1 to 16, as said below
Outputs:
- attn_out: bfloat16 [2048, 4096], P('seq', 'tp')
- key_value_cache: bfloat16 [2, 2048, 512], P(None, 'seq', 'tp')
The draws below stay inside these ranges and needn't reach their ends.
Inputs may be any that keep to these rules, and one draw needn't show every extreme that they name: `vertical_blocks`: the 16 entries of a head are distinct block indices; only the first counts[j, 0] of row j are used. `slash_offsets`: the 16 entries of a head are distinct block offsets, the first of them 0; only the first counts[j, 1] of row j are used. `counts`: column 0 is the number of used vertical blocks, column 1 the number of used slash offsets; some head uses all 16 and all 16.
All inputs are finite; a program needn't handle non-finite values.
Results may differ from the reference program's by a relative error of at most 0.0079.
Values may be sent and summed in bfloat16 or wider, within the bound.
No kernel may reach another device: no remote copies, remote signals or barrier semaphores. Data moves between devices by JAX's collectives and lax.ppermute only.
A program may use at most 128 MiB of HBM per device.

```python
import jax
import jax.numpy as jnp
from jax import lax

MODEL_WIDTH = 8192
QUERY_HEADS = 32
KEY_VALUE_HEADS = 4
HEAD_SIZE = 128
BLOCK = 64
NV = 16
NS = 16
PROMPT_TOKENS = 2048
NB = 32


def shared_key_matrix(key):
    return jax.random.normal(jax.random.fold_in(key, 7), (MODEL_WIDTH, KEY_VALUE_HEADS * HEAD_SIZE), jnp.float32) * MODEL_WIDTH ** (-0.5)


def draw_w_key(key, part):
    return shared_key_matrix(key).astype(jnp.bfloat16)


def draw_w_query(key, part):
    noise = jax.random.normal(jax.random.fold_in(key, 11), (MODEL_WIDTH, QUERY_HEADS * HEAD_SIZE), jnp.float32) * MODEL_WIDTH ** (-0.5)
    return noise.astype(jnp.bfloat16)


def vertical_row(head_key):
    return jax.random.permutation(head_key, NB)[:NV].astype(jnp.int32)


def draw_vertical_blocks(key, part):
    head_keys = jax.random.split(jax.random.fold_in(key, 3), QUERY_HEADS)
    return jax.vmap(vertical_row)(head_keys)


def slash_row(head_key):
    remaining = jax.random.permutation(head_key, NB - 1)[:NS - 1] + 1
    return jnp.concatenate([jnp.zeros((1,), jnp.int32), remaining.astype(jnp.int32)])


def draw_slash_offsets(key, part):
    head_keys = jax.random.split(jax.random.fold_in(key, 5), QUERY_HEADS)
    return jax.vmap(slash_row)(head_keys)


def draw_counts(key, part):
    vertical_used = jax.random.randint(jax.random.fold_in(key, 17), (QUERY_HEADS,), 1, NV + 1)
    slash_used = jax.random.randint(jax.random.fold_in(key, 19), (QUERY_HEADS,), 1, NS + 1)
    busiest = jax.random.randint(jax.random.fold_in(key, 23), (), 0, QUERY_HEADS)
    vertical_used = vertical_used.at[busiest].set(NV)
    slash_used = slash_used.at[busiest].set(NS)
    return jnp.stack([vertical_used, slash_used], axis=1).astype(jnp.int32)


def block_scale(own_key, extent, pieces, smallest, top_value):
    factor_of = 1.0
    for dim, parts in pieces:
        heights = jax.random.uniform(jax.random.fold_in(jax.random.fold_in(own_key, 6), dim), (parts,), jnp.float32, smallest / len(pieces), top_value / len(pieces))
        factor_of = factor_of * jnp.repeat(jnp.exp(heights), extent[dim] // parts).reshape((-1,) + (1,) * (len(extent) - 1 - dim))
    return factor_of


def centred(stream_key, extent, spread, limit, cuts=(), kind=jnp.bfloat16):
    values = jax.random.normal(stream_key, extent, jnp.float32) * spread
    if len(cuts) > 0:
        values = block_scale(stream_key, extent, cuts, -0.22, 0.18) * values
    return jnp.clip(values, min=-limit, max=limit).astype(kind)


def setup_inputs(seed: int = 0) -> dict:
    keys = jax.random.split(jax.random.key(seed), 9)
    return {
        "hidden": centred(keys[0], (PROMPT_TOKENS, MODEL_WIDTH), 1.0, 6.0, ((0, 8), (1, 4))),
        "norm_gain": jnp.clip(1.0 + 0.18 * jax.random.normal(keys[1], (MODEL_WIDTH,), jnp.float32), 0.1, 1.9),
        "w_query": draw_w_query(jax.random.fold_in(keys[8], 71), 0),
        "w_key": draw_w_key(jax.random.fold_in(keys[8], 71), 0),
        "value_weight": centred(keys[4], (MODEL_WIDTH, KEY_VALUE_HEADS * HEAD_SIZE), MODEL_WIDTH ** -0.5, 0.0625, ((0, 8), (1, 4))),
        "vertical_blocks": draw_vertical_blocks(jax.random.fold_in(keys[8], 71), 0),
        "slash_offsets": draw_slash_offsets(jax.random.fold_in(keys[8], 71), 0),
        "counts": draw_counts(jax.random.fold_in(keys[8], 71), 0),
    }


EPSILON = 1e-06
THETA = 1000000.0
NEGATIVE = -1e+30

def apply_rotary(value_rows, token_positions, head_width):
    half_width = head_width // 2
    inv_freq = THETA ** (-(jnp.arange(half_width, dtype=jnp.float32) * 2.0) / head_width)
    angles = token_positions.astype(jnp.float32)[:, None] * inv_freq[None, :]
    cosine = jnp.cos(angles)[:, None, :]
    sine_wave = jnp.sin(angles)[:, None, :]
    first_half = value_rows[..., :half_width]
    second = value_rows[..., half_width:]
    return jnp.concatenate([first_half * cosine - second * sine_wave, second * cosine + first_half * sine_wave], axis=-1)

def candidates(blocks, head_ids, vertical_blocks, slash_offsets, counts):
    verticals = vertical_blocks[head_ids]
    slashes = slash_offsets[head_ids]
    vertical_count = counts[head_ids, 0]
    slash_count = counts[head_ids, 1]
    slash_live = jnp.arange(slashes.shape[1], dtype=jnp.int32)[None, :] < slash_count[:, None]
    slash_rows = blocks[:, None] - slashes
    slash_ok = slash_live & (slash_rows >= 0)
    repeated = jnp.any((blocks[:, None, None] - verticals[:, :, None] == slashes[:, None, :]) & slash_live[:, None, :], axis=2)
    vertical_ok = (jnp.arange(verticals.shape[1], dtype=jnp.int32)[None, :] < vertical_count[:, None]) & jnp.logical_not(repeated)
    key_blocks = jnp.concatenate([verticals, jnp.maximum(slash_rows, 0)], axis=1)
    block_live = jnp.concatenate([vertical_ok, slash_ok], axis=1)
    return (key_blocks, block_live)

def attend(queries, starts, head_ids, keys_all, values_all, vertical_blocks, slash_offsets, counts):
    unit_count, row_count, head_width = queries.shape
    key_blocks, block_live = candidates(starts // BLOCK, head_ids, vertical_blocks, slash_offsets, counts)
    offsets = jnp.arange(BLOCK, dtype=jnp.int32)
    key_pos = (key_blocks[:, :, None] * BLOCK + offsets[None, None, :]).reshape(unit_count, -1)
    key_live = jnp.repeat(block_live, BLOCK, axis=1)
    query_pos = starts[:, None] + jnp.arange(row_count, dtype=jnp.int32)[None, :]
    allowed = key_live[:, None, :] & (key_pos[:, None, :] <= query_pos[:, :, None])
    picked_keys = jnp.take(keys_all, key_pos, axis=0)
    picked_values = jnp.take(values_all, key_pos, axis=0)
    scores = jnp.einsum('uqd,ukd->uqk', queries.astype(jnp.float32), picked_keys.astype(jnp.float32)) * head_width ** (-0.5)
    masked = jnp.where(allowed, scores, NEGATIVE)
    row_max = lax.optimization_barrier(jnp.max(masked, axis=-1, keepdims=True))
    weights = jnp.where(allowed, jnp.exp(masked - row_max), 0.0)
    row_sum = lax.optimization_barrier(jnp.sum(weights, axis=-1, keepdims=True))
    weights_low = lax.optimization_barrier(weights.astype(jnp.bfloat16)).astype(jnp.float32)
    blended = jnp.einsum('uqk,ukd->uqd', weights_low, picked_values.astype(jnp.float32))
    return (blended / row_sum).astype(jnp.bfloat16)

def reference(hidden, norm_gain, w_query, w_key, value_weight, vertical_blocks, slash_offsets, counts):
    widened = hidden.astype(jnp.float32)
    inv_rms = lax.rsqrt(lax.optimization_barrier(jnp.mean(widened * widened, axis=-1, keepdims=True)) + EPSILON)
    normed = (widened * inv_rms * norm_gain[None, :]).astype(jnp.bfloat16)
    query_proj = jnp.dot(normed, w_query, preferred_element_type=jnp.float32)
    key_projected = jnp.dot(normed, w_key, preferred_element_type=jnp.float32)
    value_projected = jnp.dot(normed, value_weight, preferred_element_type=jnp.float32)
    token_positions = jnp.arange(PROMPT_TOKENS, dtype=jnp.int32)
    queries = apply_rotary(query_proj.reshape(PROMPT_TOKENS, QUERY_HEADS, HEAD_SIZE), token_positions, HEAD_SIZE).astype(jnp.bfloat16)
    key_rows = apply_rotary(key_projected.reshape(PROMPT_TOKENS, KEY_VALUE_HEADS, HEAD_SIZE), token_positions, HEAD_SIZE).astype(jnp.bfloat16)
    value_rows = value_projected.reshape(PROMPT_TOKENS, KEY_VALUE_HEADS, HEAD_SIZE).astype(jnp.bfloat16)
    key_value_cache = jnp.stack([key_rows.reshape(PROMPT_TOKENS, KEY_VALUE_HEADS * HEAD_SIZE), value_rows.reshape(PROMPT_TOKENS, KEY_VALUE_HEADS * HEAD_SIZE)])
    group_width = QUERY_HEADS // KEY_VALUE_HEADS
    per_step = 8

    def one_head(head):
        head_queries = lax.dynamic_index_in_dim(queries, head, 1, keepdims=False)
        kv_head = (head // group_width).astype(jnp.int32)
        head_keys = lax.dynamic_index_in_dim(key_rows, kv_head, 1, keepdims=False)
        head_values = lax.dynamic_index_in_dim(value_rows, kv_head, 1, keepdims=False)
        units = head_queries.reshape(NB // per_step, per_step, BLOCK, HEAD_SIZE)
        starts = (jnp.arange(NB, dtype=jnp.int32) * BLOCK).reshape(NB // per_step, per_step)

        def one_group(packed):
            head_ids = jnp.zeros((per_step,), jnp.int32) + head
            return attend(packed[0], packed[1], head_ids, head_keys, head_values, vertical_blocks, slash_offsets, counts)
        return lax.map(one_group, (units, starts)).reshape(PROMPT_TOKENS, HEAD_SIZE)
    result = lax.map(one_head, jnp.arange(QUERY_HEADS, dtype=jnp.int32))
    attn_out = jnp.transpose(result, (1, 0, 2)).reshape(PROMPT_TOKENS, QUERY_HEADS * HEAD_SIZE)
    return (attn_out, key_value_cache)
```

```python
import functools

import jax
import jax.numpy as jnp
from jax import lax
from jax.experimental import pallas as pl
from jax.experimental.pallas import tpu as pltpu
from jax.sharding import PartitionSpec as P

BLOCK = 64


EPSILON = 1e-06
THETA = 1000000.0
NEGATIVE = -1e30


def apply_rotary(value_rows, token_positions, head_width):
    half_width = head_width // 2
    inv_freq = THETA ** (-(jnp.arange(half_width, dtype=jnp.float32) * 2.0) / head_width)
    angles = token_positions.astype(jnp.float32)[:, None] * inv_freq[None, :]
    cosine = jnp.cos(angles)[:, None, :]
    sine_wave = jnp.sin(angles)[:, None, :]
    first_half = value_rows[..., :half_width]
    second = value_rows[..., half_width:]
    return jnp.concatenate(
        [first_half * cosine - second * sine_wave, second * cosine + first_half * sine_wave],
        axis=-1,
    )


def lookup(table_values, head_ids):
    matches = head_ids[:, None] == jnp.arange(table_values.shape[0], dtype=jnp.int32)[None, :]
    return jnp.sum(jnp.where(matches[:, :, None], table_values[None, :, :], 0), axis=1)


def candidates(blocks, head_ids, vertical_blocks, slash_offsets, counts):
    verticals = lookup(vertical_blocks, head_ids)
    slashes = lookup(slash_offsets, head_ids)
    used = lookup(counts, head_ids)
    slash_live = jnp.arange(slashes.shape[1], dtype=jnp.int32)[None, :] < used[:, 1:2]
    slash_rows = blocks[:, None] - slashes
    slash_ok = slash_live & (slash_rows >= 0)
    repeated = jnp.any(
        (blocks[:, None, None] - verticals[:, :, None] == slashes[:, None, :])
        & slash_live[:, None, :],
        axis=2,
    )
    vertical_ok = (
        jnp.arange(verticals.shape[1], dtype=jnp.int32)[None, :] < used[:, 0:1]
    ) & jnp.logical_not(repeated)
    key_blocks = jnp.concatenate([verticals, jnp.maximum(slash_rows, 0)], axis=1)
    block_live = jnp.concatenate([vertical_ok, slash_ok], axis=1)
    return (key_blocks, block_live)


def attend(queries, starts, head_ids, block_table, vertical_blocks, slash_offsets, counts):
    unit_count, row_count, head_width = queries.shape
    key_blocks, block_live = candidates(
        starts // BLOCK, head_ids, vertical_blocks, slash_offsets, counts
    )
    offsets = jnp.arange(BLOCK, dtype=jnp.int32)
    key_pos = (key_blocks[:, :, None] * BLOCK + offsets[None, None, :]).reshape(unit_count, -1)
    key_live = jnp.repeat(block_live, BLOCK, axis=1)
    query_pos = starts[:, None] + jnp.arange(row_count, dtype=jnp.int32)[None, :]
    allowed = key_live[:, None, :] & (key_pos[:, None, :] <= query_pos[:, :, None])
    picked = jnp.take(block_table, key_blocks, axis=0).reshape(unit_count, -1, 2 * head_width)
    picked_keys = picked[:, :, :head_width]
    picked_values = picked[:, :, head_width:]
    scores = jnp.einsum(
        "uqd,ukd->uqk", queries, picked_keys, preferred_element_type=jnp.float32
    ) * head_width ** (-0.5)
    masked = jnp.where(allowed, scores, NEGATIVE)
    row_max = jnp.max(masked, axis=-1, keepdims=True)
    weights = jnp.where(allowed, jnp.exp(masked - row_max), 0.0)
    row_sum = jnp.sum(weights, axis=-1, keepdims=True)
    blended = jnp.einsum(
        "uqk,ukd->uqd",
        weights.astype(jnp.bfloat16),
        picked_values,
        preferred_element_type=jnp.float32,
    )
    return (blended / row_sum).astype(jnp.bfloat16)


def attend_all(
    queries, starts, head_ids, keys_all, values_all, vertical_blocks, slash_offsets, counts
):
    unit_count, unit_rows, head_width = queries.shape
    group_units = max(1, min(unit_count, 512 // unit_rows))
    step_count = unit_count // group_units
    block_table = jnp.concatenate([keys_all, values_all], axis=1).reshape(-1, BLOCK, 2 * head_width)

    def one_group(packed):
        return attend(
            packed[0], packed[1], packed[2], block_table, vertical_blocks, slash_offsets, counts
        )

    result = lax.map(
        one_group,
        (
            queries.reshape(step_count, group_units, unit_rows, head_width),
            starts.reshape(step_count, group_units),
            head_ids.reshape(step_count, group_units),
        ),
    )
    return result.reshape(unit_count, unit_rows, head_width)


def body(hidden, norm_gain, w_query, w_key, value_weight, vertical_blocks, slash_offsets, counts):
    features_all = lax.all_gather(hidden, "tp", axis=1, tiled=True)
    tok_rows = features_all.shape[0]
    widened = features_all.astype(jnp.float32)
    inv_rms = lax.rsqrt(jnp.mean(widened * widened, axis=-1, keepdims=True) + EPSILON)
    normed = (widened * inv_rms * norm_gain[None, :]).astype(jnp.bfloat16)
    head_width = w_key.shape[1]
    heads_here = w_query.shape[1] // head_width
    pieces = (
        lax.all_gather(w_query, "seq", axis=0, tiled=True),
        lax.all_gather(w_key, "seq", axis=0, tiled=True),
        lax.all_gather(value_weight, "seq", axis=0, tiled=True),
    )
    query_proj, key_projected, value_projected = tuple(
        (jnp.dot(normed, panel, preferred_element_type=jnp.float32) for panel in pieces)
    )
    device = lax.axis_index("seq")
    token_positions = device * tok_rows + jnp.arange(tok_rows, dtype=jnp.int32)
    queries = apply_rotary(
        query_proj.reshape(tok_rows, heads_here, head_width), token_positions, head_width
    ).astype(jnp.bfloat16)
    keys_here = (
        apply_rotary(key_projected.reshape(tok_rows, 1, head_width), token_positions, head_width)
        .reshape(tok_rows, head_width)
        .astype(jnp.bfloat16)
    )
    values_here = value_projected.astype(jnp.bfloat16)
    key_value_cache = jnp.stack([keys_here, values_here])
    keys_all, values_all = (
        lax.all_gather(keys_here, "seq", axis=0, tiled=True),
        lax.all_gather(values_here, "seq", axis=0, tiled=True),
    )
    group_base = lax.axis_index("tp") * heads_here
    block_count = tok_rows // BLOCK
    units = jnp.transpose(
        queries.reshape(block_count, BLOCK, heads_here, head_width), (2, 0, 1, 3)
    ).reshape(heads_here * block_count, BLOCK, head_width)
    local_starts = device * tok_rows + jnp.arange(block_count, dtype=jnp.int32) * BLOCK
    starts = jnp.tile(local_starts, heads_here)
    head_ids = group_base + jnp.repeat(jnp.arange(heads_here, dtype=jnp.int32), block_count)
    result = attend_all(
        units, starts, head_ids, keys_all, values_all, vertical_blocks, slash_offsets, counts
    )
    attn_out = jnp.transpose(
        result.reshape(heads_here, block_count, BLOCK, head_width), (1, 2, 0, 3)
    ).reshape(tok_rows, heads_here * head_width)
    return (attn_out, key_value_cache)


AXES = ("seq", "tp")
LANES = 128


def pairs(n_tp, move):
    out = []
    for seq in range(8):
        for tp in range(n_tp):
            zh, zl, x, y, c = seq >> 2, (seq >> 1) & 1, seq & 1, tp >> 1, tp & 1
            zh, zl, x, y, c = move(zh, zl, x, y, c)
            out.append((seq * n_tp + tp, (zh * 4 + zl * 2 + x) * n_tp + y * 2 + c))
    return out


def send(value, n_tp, move):
    return lax.ppermute(value, AXES, pairs(n_tp, move))


def flip_x(zh, zl, x, y, c):
    return zh, zl, 1 - x, y, c


def flip_y(zh, zl, x, y, c):
    return zh, zl, x, 1 - y, c


def flip_c(zh, zl, x, y, c):
    return zh, zl, x, y, 1 - c


def flip_zl(zh, zl, x, y, c):
    return zh, 1 - zl, x, y, c


def flip_zh(zh, zl, x, y, c):
    return 1 - zh, zl, x, y, c


def spread(i, j):
    return lambda zh, zl, x, y, c: (zh ^ i, c, x ^ j, y, zl ^ c)


def prepare_kernel(where, hidden, gain, kept, sent, squares):
    rows = kept.shape[0]
    wide = hidden[...].astype(jnp.float32)
    total = jnp.sum(wide * wide, axis=1, keepdims=True)
    squares[...] = jnp.broadcast_to(total, squares.shape)
    y = where[3]
    for half, target in ((y, kept), (1 - y, sent)):
        part = hidden[pl.ds(pl.multiple_of(half * rows, rows), rows), :].astype(jnp.float32)
        target[...] = (part * gain[0]).astype(target.dtype)


def prepare(where, hidden, norm_gain):
    rows, width = hidden.shape
    gains = norm_gain.reshape(-1, 1, width)
    half = jax.ShapeDtypeStruct((rows // 2, width), hidden.dtype)
    return pl.pallas_call(
        prepare_kernel,
        grid_spec=pltpu.PrefetchScalarGridSpec(
            num_scalar_prefetch=1,
            grid=(1,),
            in_specs=[
                pl.BlockSpec((rows, width), lambda g, w: (0, 0)),
                pl.BlockSpec((1, 1, width), lambda g, w: (w[3] * 2 + w[4], 0, 0)),
            ],
            out_specs=[
                pl.BlockSpec((rows // 2, width), lambda g, w: (0, 0)),
                pl.BlockSpec((rows // 2, width), lambda g, w: (0, 0)),
                pl.BlockSpec((rows, LANES), lambda g, w: (0, 0)),
            ],
        ),
        out_shape=[half, half, jax.ShapeDtypeStruct((rows, LANES), jnp.float32)],
        name="prepare",
    )(where, hidden, gains)


def pieces_kernel(where, own, other, *outs):
    width = outs[0].shape[1]
    zh, x, y = where[0], where[2], where[3]
    for i in range(2):
        for j in range(2):
            col = pl.ds(pl.multiple_of((x ^ j) * width, width), width)
            out = outs[2 * i + j]

            @pl.when((zh ^ i) == y)
            def _(out=out, col=col):
                out[...] = own[:, col]

            @pl.when((zh ^ i) != y)
            def _(out=out, col=col):
                out[...] = other[:, col]


def pieces(where, own, other):
    rows, width = own.shape
    block = pl.BlockSpec((rows, width // 2), lambda g, w: (0, 0))
    full = pl.BlockSpec((rows, width), lambda g, w: (0, 0))
    return pl.pallas_call(
        pieces_kernel,
        grid_spec=pltpu.PrefetchScalarGridSpec(
            num_scalar_prefetch=1, grid=(1,), in_specs=[full, full], out_specs=[block] * 4
        ),
        out_shape=[jax.ShapeDtypeStruct((rows, width // 2), own.dtype)] * 4,
        name="pieces",
    )(where, own, other)


def join_kernel(*refs):
    out = refs[-1]
    for n, ref in enumerate(refs[:-1]):
        out[n] = ref[...]


def join(parts):
    shape = (len(parts),) + parts[0].shape
    return pl.pallas_call(
        join_kernel, out_shape=jax.ShapeDtypeStruct(shape, parts[0].dtype), name="join"
    )(*parts)


def project_kernel(where, own, other, wq, wk, wv, *outs):
    c = where[4]
    u = pl.program_id(0)
    rows, depth = own.shape[2:]

    def work(src):
        a = src[...].reshape(2 * rows, depth)
        kv = jnp.concatenate(
            [
                jnp.dot(a, wk[...], preferred_element_type=jnp.float32),
                jnp.dot(a, wv[...], preferred_element_type=jnp.float32),
            ],
            axis=1,
        )
        parts = [kv]
        chunks = len(outs) // 2 - 1
        span = wq.shape[1] // chunks
        for n in range(chunks):
            parts.append(
                jnp.dot(
                    a, wq[:, n * span : (n + 1) * span], preferred_element_type=jnp.float32
                )
            )
        for n, part in enumerate(parts):
            outs[2 * n][0, 0] = part[:rows]
            outs[2 * n + 1][0, 0] = part[rows:].astype(jnp.bfloat16)

    @pl.when(u == c)
    def _():
        work(own)

    @pl.when(u != c)
    def _():
        work(other)


def project(where, own, other, w_query, w_key, value_weight, chunks):
    rows, depth = own.shape[1:]
    own = own.reshape(2, 2, rows, depth)
    other = other.reshape(2, 2, rows, depth)
    a_spec = pl.BlockSpec((1, 2, rows, depth), lambda u, i, w: (i, 0, 0, 0))
    whole = lambda v: pl.BlockSpec(v.shape, lambda u, i, w: (0, 0))
    widths = [w_key.shape[1] + value_weight.shape[1]] + [w_query.shape[1] // chunks] * chunks
    out_specs, out_shape = [], []
    for width in widths:
        for kind in (jnp.float32, jnp.bfloat16):
            out_specs.append(pl.BlockSpec((1, 1, rows, width), lambda u, i, w: (u, i, 0, 0)))
            out_shape.append(jax.ShapeDtypeStruct((2, 2, rows, width), kind))
    flat = pl.pallas_call(
        project_kernel,
        grid_spec=pltpu.PrefetchScalarGridSpec(
            num_scalar_prefetch=1,
            grid=(2, 2),
            in_specs=[a_spec, a_spec, whole(w_query), whole(w_key), whole(value_weight)],
            out_specs=out_specs,
        ),
        out_shape=out_shape,
        name="project",
    )(where, own, other, w_query, w_key, value_weight)
    return [(flat[2 * n], flat[2 * n + 1]) for n in range(len(widths))]


def reduce_chunk(n_tp, keep, sent):
    wide = jnp.float32
    total = keep + send(sent, n_tp, flip_x).astype(wide)
    total = total[0] + send(total[1].astype(jnp.bfloat16), n_tp, flip_zl).astype(wide)
    return total[0] + send(total[1].astype(jnp.bfloat16), n_tp, flip_zh).astype(wide)


def rope_angles(token_positions, head_width):
    half_width = head_width // 2
    inv_freq = THETA ** (-(jnp.arange(half_width, dtype=jnp.float32) * 2.0) / head_width)
    angles = token_positions.astype(jnp.float32)[:, None] * inv_freq[None, :]
    cosine, sine = jnp.cos(angles), jnp.sin(angles)
    return jnp.concatenate([cosine, cosine], 1), jnp.concatenate([-sine, sine], 1)


def turn(rows, cosine, sine):
    half = rows.shape[-1] // 2
    swapped = jnp.concatenate([rows[..., half:], rows[..., :half]], axis=-1)
    return rows * cosine + swapped * sine


def block_bounds(first_block, count, total_blocks, head_ids, verticals, slashes, counts):
    verticals, slashes = lookup(verticals, head_ids), lookup(slashes, head_ids)
    used = lookup(counts, head_ids)
    blocks = first_block + jnp.arange(count, dtype=jnp.int32)
    keys = jnp.arange(total_blocks, dtype=jnp.int32)
    slash_live = jnp.arange(slashes.shape[1], dtype=jnp.int32)[None, :] < used[:, 1:2]
    vertical_live = jnp.arange(verticals.shape[1], dtype=jnp.int32)[None, :] < used[:, 0:1]
    gap = blocks[:, None] - keys[None, :]
    by_slash = jnp.any(
        (gap[None, :, :, None] == slashes[:, None, None, :]) & slash_live[:, None, None, :], axis=3
    )
    by_vertical = jnp.any(
        (keys[None, :, None] == verticals[:, None, :]) & vertical_live[:, None, :], axis=2
    )
    allowed = (by_slash | by_vertical[:, None, :]) & (gap >= 0)[None]
    return jnp.repeat(jnp.where(allowed, jnp.finfo(jnp.float32).max, NEGATIVE), BLOCK, axis=2)


def attend_kernel(where, q, cosine, sine, scale, k, v, bounds, out):
    rows, width = q.shape
    total = k.shape[0]
    first = where[5]
    query = turn(q[...] * scale[...], cosine[...], sine[...]).astype(jnp.bfloat16)
    scores = lax.dot_general(
        query, k[...], (((1,), (1,)), ((), ())), preferred_element_type=jnp.float32
    )
    count = rows // BLOCK
    bound = jnp.concatenate(
        [jnp.broadcast_to(bounds[0, n : n + 1, :], (BLOCK, total)) for n in range(count)], axis=0
    )
    key_pos = lax.broadcasted_iota(jnp.int32, (rows, total), 1)
    query_pos = lax.broadcasted_iota(jnp.int32, (rows, total), 0) + first
    scores = jnp.where(key_pos <= query_pos, jnp.minimum(scores, bound), NEGATIVE)
    top = jnp.max(scores, axis=1, keepdims=True)
    weights = jnp.exp((scores - top) * width ** (-0.5))
    row_sum = jnp.sum(weights, axis=1, keepdims=True)
    blended = jnp.dot(weights.astype(jnp.bfloat16), v[...], preferred_element_type=jnp.float32)
    out[...] = (blended / row_sum).astype(out.dtype)


def attend_dense(where, q, cosine, sine, scale, k, v, bounds):
    rows, columns = q.shape
    total, width = k.shape
    heads = columns // width
    flat = lambda a: pl.BlockSpec(a.shape, lambda h, w: (0, 0))
    return pl.pallas_call(
        attend_kernel,
        grid_spec=pltpu.PrefetchScalarGridSpec(
            num_scalar_prefetch=1,
            grid=(heads,),
            in_specs=[
                pl.BlockSpec((rows, width), lambda h, w: (0, h)),
                flat(cosine),
                flat(sine),
                flat(scale),
                flat(k),
                flat(v),
                pl.BlockSpec((1,) + bounds.shape[1:], lambda h, w: (h, 0, 0)),
            ],
            out_specs=pl.BlockSpec((rows, width), lambda h, w: (0, h)),
        ),
        out_shape=jax.ShapeDtypeStruct((rows, columns), jnp.bfloat16),
        name="attend",
    )(where, q, cosine, sine, scale, k, v, bounds)


def in_place(
    n_tp, hidden, norm_gain, w_query, w_key, value_weight, vertical_blocks, slash_offsets, counts
):
    rows = hidden.shape[0]
    head_width = w_key.shape[1]
    heads_here = w_query.shape[1] // head_width
    total = rows * lax.axis_size("seq")
    seq, tp = lax.axis_index("seq"), lax.axis_index("tp")
    y, c = tp >> 1, tp & 1
    where = jnp.stack([seq >> 2, (seq >> 1) & 1, seq & 1, y, c, seq * rows]).astype(jnp.int32)

    own, away, squares = prepare(where, hidden, norm_gain)
    other = send(away, n_tp, flip_y)
    parts = pieces(where, own, other)
    q0 = join([send(parts[2 * i + j], n_tp, spread(i, j)) for i in range(2) for j in range(2)])
    q1 = send(q0, n_tp, flip_c)
    q2 = send(q0, n_tp, flip_y)
    q3 = send(q2, n_tp, flip_c)
    squares = squares + send(squares, n_tp, flip_c)
    squares = squares + send(squares, n_tp, flip_y)
    scale = lax.rsqrt(squares / norm_gain.shape[0] + EPSILON)

    chunks = 2
    near = project(where, q0, q1, w_query, w_key, value_weight, chunks)
    far = project(where, q2, q3, w_query, w_key, value_weight, chunks)

    def whole(n):
        mine = reduce_chunk(n_tp, *near[n])
        theirs = reduce_chunk(n_tp, *far[n])
        return jnp.where(
            y == 0,
            jnp.concatenate([mine, theirs], axis=0),
            jnp.concatenate([theirs, mine], axis=0),
        )

    cosine, sine = rope_angles(
        seq * rows + jnp.arange(rows, dtype=jnp.int32), head_width
    )
    kv = whole(0) * scale[:, :1]
    keys_here = turn(kv[:, :head_width], cosine, sine).astype(jnp.bfloat16)
    values_here = kv[:, head_width:].astype(jnp.bfloat16)
    key_value_cache = jnp.stack([keys_here, values_here])

    gathered = key_value_cache[None]
    for move in (flip_zh, flip_zl, flip_x):
        gathered = jnp.stack([gathered, send(gathered, n_tp, move)])
    gathered = gathered[:, :, :, 0]
    for axis, digit in ((0, seq & 1), (1, (seq >> 1) & 1), (2, seq >> 2)):
        gathered = jnp.where(digit == 0, gathered, jnp.flip(gathered, axis))
    gathered = jnp.transpose(gathered, (3, 2, 1, 0, 4, 5)).reshape(2, total, head_width)

    head_ids = tp * heads_here + jnp.arange(heads_here, dtype=jnp.int32)
    bounds = block_bounds(
        seq * (rows // BLOCK),
        rows // BLOCK,
        total // BLOCK,
        head_ids,
        vertical_blocks,
        slash_offsets,
        counts,
    )
    queries = jnp.concatenate([whole(n + 1) for n in range(chunks)], axis=1)
    attn_out = attend_dense(
        where, queries, cosine, sine, scale, gathered[0], gathered[1], bounds
    )
    return (attn_out, key_value_cache)


def solution(mesh):
    in_specs = (P("seq", "tp"), P(), P("seq", "tp"), P("seq", "tp"), P("seq", "tp"), P(), P(), P())
    out_specs = (P("seq", "tp"), P(None, "seq", "tp"))
    n_seq, n_tp = mesh.shape["seq"], mesh.shape["tp"]
    work = body
    if (n_seq.bit_length(), n_tp.bit_length()) == (4, 3) and n_seq == 2 * n_tp:
        work = functools.partial(in_place, n_tp)
    return jax.shard_map(work, mesh=mesh, in_specs=in_specs, out_specs=out_specs, check_vma=False)
```
